32 devices in a mesh: grp: 2 (over y), mon: 4 (over z), pair: 2 (over x), sub: 2 (over core).
Axes of the slice: x: 2, y: 2, z: 4, core: 2. Of those that a mesh axis runs over, the one named last changes fastest.
Arguments:
- dfactors: bfloat16 [8192, 1024], P('mon', 'sub'), may hold values from -0.5 to 0.5
- block_mask: int32 [64, 1024], P('mon', 'sub'), may hold values 0 or 1
- base_flow: float32 [8192], P('mon'), may hold values from -5 to 5
- branch_row: int32 [1024], replicated, may hold values from 0 to 8191, as said below
- pair_slots: int32 [3072, 2], P(('grp', 'pair')), parts along dimension 0, may hold values from 0 to 1023, as said below
- pair_counts: int32 [4], P(('grp', 'pair')), parts along dimension 0, may hold values from 1 to 768, 1024 in all
Outputs:
- post_flows: bfloat16 [8192, 3072], P(('mon', 'sub'), ('grp', 'pair')), parts along dimension 1
The draws below stay inside these ranges and needn't reach their ends.
There are 2 independent parts, one for each index of `grp`. The reference program is written for one: setup_inputs(seed, part) draws one part's arguments, and reference() takes and returns one part's arrays. A program takes and returns all parts, laid end to end along the dimension named above; an argument that names none is the same for every part. Nothing has to cross between parts.
Inputs may be any that keep to these rules, and one draw needn't show every extreme that they name: `branch_row`: all entries distinct. `pair_slots`: the two candidates of a slot differ; empty slots hold valid pairs too. `pair_counts`: the counts sum to 1024; an owner's live slots are its first ones.
All inputs are finite; a program needn't handle non-finite values. No bound on the sum of `block_mask` or of `pair_counts` on one device may be relied on, other than what follows from the above.
Results may differ from the reference program's by a relative error of at most 0.004.
Values may be sent and summed in bfloat16 or wider, within the bound.
A program may use at most 64 MiB of HBM per device.

```python
import math
import jax
import jax.numpy as jnp
import numpy as np
from jax import lax

BLOCK = 128
C = 1024
MB_DEV = 16
M = 8192
PAIRS = 1024
PCAP = 768
SLOTS = 1536
N_MON = 4
N_PAIR = 2
N_SUB = 2


def draw_branch_row(key, part):
    return jax.random.permutation(jax.random.fold_in(key, 11), M)[:C].astype(jnp.int32)


def draw_pair_slots(key, part):
    first_out = jax.random.randint(jax.random.fold_in(key, 21), (SLOTS,), 0, C)
    offset_draw = jax.random.randint(jax.random.fold_in(key, 22), (SLOTS,), 1, C)
    second_out = (first_out + offset_draw) % C
    first_out = first_out.at[0].set(C - 1)
    second_out = second_out.at[0].set(0)
    return jnp.stack([first_out, second_out], axis=1).astype(jnp.int32)


def place_ends(drawn, stream_key, least, high):
    spot = [jax.random.randint(jax.random.fold_in(stream_key, axis), (), 0, length) for axis, length in enumerate(drawn.shape)]
    widest = drawn.shape.index(max(drawn.shape))
    next_to = spot[:widest] + [(spot[widest] + 1) % drawn.shape[widest]] + spot[widest + 1:]
    return drawn.at[tuple(spot)].set(least).at[tuple(next_to)].set(high)


def shard_levels(own_key, extent, shards, smallest, top_value):
    def one(dim, blocks):
        heights = jax.random.uniform(jax.random.fold_in(jax.random.fold_in(own_key, 6), dim), (blocks,), jnp.float32, smallest / len(shards), top_value / len(shards))
        return jnp.repeat(jnp.exp(heights), extent[dim] // blocks).reshape((-1,) + (1,) * (len(extent) - dim - 1))

    gain = one(*shards[0])
    for cut in shards[1:]:
        gain = gain * one(*cut)
    return gain


def length_profile(amount, total, most, skew):
    weights = [(1 << 20) // math.isqrt(grade ** skew) + 1 for grade in range(2, amount + 1)]
    spare, given = total - most - (amount - 1), [1] * (amount - 1)
    while spare > 0:
        free = [i for i in range(amount - 1) if given[i] < most]
        whole, left = sum([weights[i] for i in free]), spare
        for i in free:
            more = min(most - given[i], max(1, left * weights[i] // whole), spare)
            given[i] = given[i] + more
            spare = spare - more
    return np.array([most] + given)


def ragged_sizes(key, amount, total, reach, slope):
    if amount == 2:
        one = jax.random.randint(key, (), max(1, total - reach), min(reach, total - 1) + 1)
        return jnp.stack([one, total - one])
    sizes = jnp.asarray(length_profile(amount, total, reach, slope), jnp.int32)
    twos = (amount - 1) // 2
    donor, sink = sizes[1:1 + 2 * twos:2], sizes[2:2 + 2 * twos:2]
    slack = jnp.minimum(donor - 1, reach - sink)
    shifted = jax.random.randint(jax.random.fold_in(key, 1), (twos,), 0, 1 << 20) % (slack + 1)
    sizes = sizes.at[1:1 + 2 * twos:2].set(donor - shifted).at[2:2 + 2 * twos:2].set(sink + shifted)
    return sizes[jax.random.permutation(jax.random.fold_in(key, 2), amount)]


def scatter_about(stream_key, extent, deviation, most, split=(), kind=jnp.bfloat16):
    drawn = jax.random.normal(stream_key, extent, jnp.float32) * deviation
    if len(split) > 0:
        drawn = shard_levels(stream_key, extent, split, -0.22, 0.18) * drawn
    return jnp.clip(drawn, min=-most, max=most).astype(kind)


def setup_inputs(seed: int = 0, part: int = 0) -> dict:
    keys = jax.random.split(jax.random.key(seed), 7)
    own_keys = jax.random.split(jax.random.fold_in(keys[6], part), 7)
    dfactors = jnp.clip(jax.random.uniform(keys[0], (M, C), jnp.float32, -0.5, 0.5) * shard_levels(keys[0], (M, C), ((0, 4), (1, 2)), -0.4, 0.0), -0.5, 0.5).astype(jnp.bfloat16)
    block_mask = place_ends((jax.random.randint(keys[1], (M // BLOCK, C), 0, 4) < 3).astype(jnp.int32), jax.random.fold_in(keys[1], 1), 0, 1)
    base_flow = scatter_about(keys[2], (M,), 1.0, 5.0, ((0, 4),), jnp.float32)
    branch_row = draw_branch_row(jax.random.fold_in(keys[6], 71), part)
    pair_slots = draw_pair_slots(jax.random.fold_in(jax.random.fold_in(keys[6], part), 71), part)
    pair_counts = ragged_sizes(own_keys[5], N_PAIR, PAIRS, PCAP, 2).astype(jnp.int32)
    return {"dfactors": dfactors, "block_mask": block_mask, "base_flow": base_flow, "branch_row": branch_row, "pair_slots": pair_slots, "pair_counts": pair_counts}


def reference(dfactors, block_mask, base_flow, branch_row, pair_slots, pair_counts):
    col_width = C // N_SUB
    block_keep = jnp.repeat(block_mask.astype(jnp.bfloat16), BLOCK, axis=0)
    masked = dfactors * block_keep
    first_out = pair_slots[:, 0]
    second_out = pair_slots[:, 1]
    first_row = branch_row[first_out]
    second_row = branch_row[second_out]
    cross_first = masked[first_row, second_out].astype(jnp.float32)
    cross_second = masked[second_row, first_out].astype(jnp.float32)
    flow_first = base_flow[first_row]
    flow_second = base_flow[second_row]
    determinant = 1.0 - cross_first * cross_second
    shift_first = (flow_first + cross_first * flow_second) / determinant
    shift_second = (flow_second + cross_second * flow_first) / determinant
    columns = jnp.arange(C, dtype=jnp.int32)[:, None]
    shift = (jnp.where(columns == first_out[None, :], shift_first[None, :], jnp.float32(0.0))
             + jnp.where(columns == second_out[None, :], shift_second[None, :], jnp.float32(0.0))).astype(jnp.bfloat16)
    slot_ids = jnp.arange(SLOTS, dtype=jnp.int32)
    live_slot = ((slot_ids % PCAP) < pair_counts[slot_ids // PCAP]).astype(jnp.float32)
    row_blocks = masked.reshape(N_MON, MB_DEV * BLOCK, C)
    flow_blocks = base_flow.reshape(N_MON, MB_DEV * BLOCK)

    def one_block(inputs):
        rows_here, flows_here = inputs
        total = jnp.zeros((rows_here.shape[0], SLOTS), jnp.float32)
        for which in range(N_SUB):
            partial_value = jnp.dot(rows_here[:, which * col_width:(which + 1) * col_width],
                              shift[which * col_width:(which + 1) * col_width],
                              preferred_element_type=jnp.float32).astype(jnp.bfloat16)
            total = total + lax.optimization_barrier(partial_value).astype(jnp.float32)
        return ((flows_here[:, None] + total) * live_slot[None, :]).astype(jnp.bfloat16)

    result = lax.map(one_block, (row_blocks, flow_blocks))
    return result.reshape(M, SLOTS)
```

```python
import functools

import jax
import jax.numpy as jnp
from jax import lax
from jax.experimental import pallas as pl
from jax.experimental.pallas import tpu as pltpu
from jax.sharding import PartitionSpec as P

BLOCK = 128
MESH = pl.DeviceIdType.MESH
F32 = jnp.float32
BF16 = jnp.bfloat16
I32 = jnp.int32


def lookup(table, index):
    groups = []
    height = table.shape[0]
    for start in range(0, index.shape[1], 128):
        wide = jnp.broadcast_to(index[:, start:start + 128], (height, 128))
        lanes = jnp.take_along_axis(table, wide & 127, axis=1)
        level = lax.broadcasted_iota(I32, (height, 128), 0)
        picked = jnp.where(level == (wide >> 7), lanes, jnp.zeros_like(lanes))
        groups.append(jnp.sum(picked, axis=0, keepdims=True))
    return jnp.concatenate(groups, axis=1)


def kernel(n_mon, n_sub, chunk, df_hbm, mask_hbm, base_hbm, row_hbm, pair_hbm, count_hbm, out_hbm,
           own_df, rest_df, far_df, mask_v, far_mask, base_v, row_v, pair_v, count_s,
           base_wide, product, mask_sum, out_v, flow_own, flow_got, cross_own, cross_got,
           load_sem, part_send, part_recv, flow_send, flow_recv, cross_send, cross_recv, out_sem):
    rows_dev, width = df_hbm.shape
    half = rows_dev // n_sub
    blocks = half // BLOCK
    capacity = pair_hbm.shape[1]
    chunks = capacity // chunk
    n = n_mon * n_sub
    mon = lax.axis_index("mon")
    sub = lax.axis_index("sub")
    me = mon * n_sub + sub
    other = 1 - sub

    def peer(step):
        flat = lax.rem(me + step, n)
        return {"mon": flat // n_sub, "sub": lax.rem(flat, n_sub)}

    barrier = pltpu.get_barrier_semaphore()

    def greet(step, carry):
        pl.semaphore_signal(barrier, inc=1, device_id=peer(step), device_id_type=MESH)
        return carry

    lax.fori_loop(1, n, greet, 0)

    loads = [
        pltpu.make_async_copy(pair_hbm, pair_v, load_sem.at[0]),
        pltpu.make_async_copy(row_hbm, row_v, load_sem.at[1]),
        pltpu.make_async_copy(df_hbm.at[pl.ds(sub * half, half)], own_df, load_sem.at[2]),
        pltpu.make_async_copy(base_hbm.at[pl.ds(sub * blocks, blocks)], base_v, load_sem.at[3]),
        pltpu.make_async_copy(df_hbm.at[pl.ds(other * half, half)], rest_df.at[pl.ds(0, half)], load_sem.at[4]),
        pltpu.make_async_copy(mask_hbm, mask_v, load_sem.at[5]),
        pltpu.make_async_copy(count_hbm, count_s, load_sem.at[6]),
    ]
    for load in loads:
        load.start()
    loads[0].wait()
    loads[1].wait()
    loads[3].wait()
    table = row_v[...]
    base = base_v[...]
    first, second = pair_v[0:1, :], pair_v[1:2, :]
    first_row, second_row = lookup(table, first), lookup(table, second)
    row_start = mon * rows_dev
    flow_start = row_start + sub * half
    flow_own[0:1, :] = lookup(base, first_row - flow_start)
    flow_own[1:2, :] = lookup(base, second_row - flow_start)
    for b in range(blocks):
        base_wide[b * BLOCK:(b + 1) * BLOCK, :] = jnp.broadcast_to(base[b:b + 1, :], (BLOCK, BLOCK)).T

    pl.semaphore_wait(barrier, n - 1)
    partner = {"sub": other}
    part_copies = [
        pltpu.make_async_remote_copy(
            df_hbm.at[pl.ds(other * half, half)], far_df.at[pl.ds(0, half)],
            part_send.at[0], part_recv.at[0], device_id=partner, device_id_type=MESH),
        pltpu.make_async_remote_copy(
            mask_hbm.at[pl.ds(other * blocks, blocks)], far_mask,
            part_send.at[1], part_recv.at[1], device_id=partner, device_id_type=MESH),
    ]
    for copy in part_copies:
        copy.start()

    def send_flow(step, carry):
        pltpu.make_async_remote_copy(
            flow_own, flow_got.at[step - 1], flow_send, flow_recv,
            device_id=peer(step), device_id_type=MESH).start()
        return carry

    lax.fori_loop(1, n, send_flow, 0)

    def send_cross(c):
        def body(step, carry):
            pltpu.make_async_remote_copy(
                cross_own.at[c], cross_got.at[c, step - 1], cross_send.at[c], cross_recv.at[c],
                device_id=peer(step), device_id_type=MESH).start()
            return carry

        lax.fori_loop(1, n, body, 0)

    def both(left, right, c):
        span = slice(c * chunk, (c + 1) * chunk)
        return jnp.concatenate([left[:, span], right[:, span]], axis=1)

    def one_hot(columns, start):
        level = lax.broadcasted_iota(I32, (width, columns.shape[1]), 0) + start
        return jnp.where(level == columns, F32(1), F32(0)).astype(BF16)

    loads[5].wait()
    rest_df[half:, :] = mask_v[...].astype(F32).astype(BF16)
    loads[2].wait()
    loads[4].wait()
    level = lax.broadcasted_iota(I32, (half, 2 * chunk), 0)
    level16 = lax.broadcasted_iota(I32, (n_sub * blocks, 2 * chunk), 0)
    for c in range(chunks):
        columns = both(first, second, c)
        wanted = both(second_row, first_row, c) - row_start
        hot = one_hot(columns, sub * width)
        near = jnp.dot(own_df[...], hot, preferred_element_type=F32)
        product[c] = near.astype(BF16)
        found = jnp.sum(jnp.where(level == wanted - sub * half, near, F32(0)), axis=0, keepdims=True)
        rest = jnp.dot(rest_df[...], hot, preferred_element_type=F32)
        found = found + jnp.sum(
            jnp.where(level == wanted - other * half, rest[:half], F32(0)), axis=0, keepdims=True)
        kept = rest[half:]
        keep = jnp.sum(jnp.where(level16 == (wanted >> 7), kept, F32(0)), axis=0, keepdims=True)
        mask_sum[c] = jnp.where(sub == 0, kept[:blocks], kept[blocks:])
        found = found * keep
        cross_own[c, 0:1, :] = found[:, chunk:]
        cross_own[c, 1:2, :] = found[:, :chunk]
        send_cross(c)

    for copy in part_copies:
        copy.wait_recv()
    far_df[half:half + blocks, :] = far_mask[...].astype(F32).astype(BF16)
    for c in range(chunks):
        hot = one_hot(both(first, second, c), other * width)
        far = jnp.dot(far_df[...], hot, preferred_element_type=F32)
        product[c] = (product[c].astype(F32) + far[:half]).astype(BF16)
        mask_sum[c] = mask_sum[c] + far[half:half + blocks]

    pltpu.make_async_copy(flow_got, flow_got, flow_recv).wait()
    loads[6].wait()
    flow = flow_own[...] + jnp.sum(flow_got[...], axis=0)
    live = (lax.broadcasted_iota(I32, (1, capacity), 1) < count_s[0]).astype(F32)
    outs = []
    for c in range(chunks):
        span = slice(c * chunk, (c + 1) * chunk)
        pltpu.make_async_copy(cross_got.at[c], cross_got.at[c], cross_recv.at[c]).wait()
        cross = cross_own[c] + jnp.sum(cross_got[c], axis=0)
        cross_first, cross_second = cross[0:1], cross[1:2]
        flow_first, flow_second = flow[0:1, span], flow[1:2, span]
        determinant = 1.0 - cross_first * cross_second
        shift_first = (flow_first + cross_first * flow_second) / determinant
        shift_second = (flow_second + cross_second * flow_first) / determinant
        alive = live[:, span]
        shift_first = shift_first.astype(BF16).astype(F32) * alive
        shift_second = shift_second.astype(BF16).astype(F32) * alive
        keep = mask_sum[c]
        for b in range(blocks):
            rows = slice(b * BLOCK, (b + 1) * BLOCK)
            flows = jnp.concatenate([base_wide[rows, :]] * (chunk // BLOCK), axis=1)
            e1 = shift_first * keep[b:b + 1, :chunk]
            e2 = shift_second * keep[b:b + 1, chunk:]
            value = flows * alive + product[c, rows, :chunk].astype(F32) * e1
            value = value + product[c, rows, chunk:].astype(F32) * e2
            out_v[rows, span] = value.astype(BF16)
        outs.append(pltpu.make_async_copy(out_v.at[:, span], out_hbm.at[:, span], out_sem.at[c]))
        outs[-1].start()

    for copy in part_copies:
        copy.wait_send()
    pltpu.make_async_copy(flow_got, flow_got, flow_send).wait()
    for c in range(chunks):
        pltpu.make_async_copy(cross_got.at[c], cross_got.at[c], cross_send.at[c]).wait()
    for copy in outs:
        copy.wait()


def on_device(n_mon, n_sub, dfactors, block_mask, base_flow, branch_row, pair_slots, pair_counts):
    rows_dev, width = dfactors.shape
    half = rows_dev // n_sub
    blocks = half // BLOCK
    capacity = pair_slots.shape[0]
    chunk = 256 if capacity % 256 == 0 else BLOCK
    chunks = capacity // chunk
    n = n_mon * n_sub
    any_spec = pl.BlockSpec(memory_space=pltpu.HBM)
    dma = pltpu.SemaphoreType.DMA
    return pl.pallas_call(
        functools.partial(kernel, n_mon, n_sub, chunk),
        out_shape=jax.ShapeDtypeStruct((half, capacity), BF16),
        in_specs=[any_spec] * 6,
        out_specs=any_spec,
        scratch_shapes=[
            pltpu.VMEM((half, width), BF16),
            pltpu.VMEM((half + n_sub * blocks, width), BF16),
            pltpu.VMEM((half + n_sub * blocks, width), BF16),
            pltpu.VMEM((n_sub * blocks, width), I32),
            pltpu.VMEM((blocks, width), I32),
            pltpu.VMEM((blocks, BLOCK), F32),
            pltpu.VMEM((branch_row.shape[0] // BLOCK, BLOCK), I32),
            pltpu.VMEM((2, capacity), I32),
            pltpu.SMEM((1,), I32),
            pltpu.VMEM((half, BLOCK), F32),
            pltpu.VMEM((chunks, half, 2 * chunk), BF16),
            pltpu.VMEM((chunks, blocks, 2 * chunk), F32),
            pltpu.VMEM((half, capacity), BF16),
            pltpu.VMEM((2, capacity), F32),
            pltpu.VMEM((n - 1, 2, capacity), F32),
            pltpu.VMEM((chunks, 2, chunk), F32),
            pltpu.VMEM((chunks, n - 1, 2, chunk), F32),
            dma((7,)), dma((2,)), dma((2,)), dma, dma, dma((chunks,)), dma((chunks,)), dma((chunks,)),
        ],
        compiler_params=pltpu.CompilerParams(
            collective_id=0, has_side_effects=True, vmem_limit_bytes=60 * 1024 * 1024),
    )(dfactors, block_mask, base_flow.reshape(-1, BLOCK), branch_row.reshape(-1, BLOCK),
      pair_slots.T, pair_counts)


def solution(mesh):
    return jax.shard_map(
        functools.partial(on_device, mesh.shape["mon"], mesh.shape["sub"]),
        mesh=mesh,
        in_specs=(
            P("mon", "sub"),
            P("mon", "sub"),
            P("mon"),
            P(),
            P(("grp", "pair"), None),
            P(("grp", "pair")),
        ),
        out_specs=P(("mon", "sub"), ("grp", "pair")),
        check_vma=False,
    )
```

```python
import functools

import jax
import jax.numpy as jnp
from jax import lax
from jax.experimental import pallas as pl
from jax.experimental.pallas import tpu as pltpu
from jax.sharding import PartitionSpec as P

BLOCK = 128
MESH = pl.DeviceIdType.MESH
F32 = jnp.float32
BF16 = jnp.bfloat16
I32 = jnp.int32


def lookup(table, index):
    groups = []
    height = table.shape[0]
    for start in range(0, index.shape[1], 128):
        wide = jnp.broadcast_to(index[:, start:start + 128], (height, 128))
        lanes = jnp.take_along_axis(table, wide & 127, axis=1)
        level = lax.broadcasted_iota(I32, (height, 128), 0)
        picked = jnp.where(level == (wide >> 7), lanes, jnp.zeros_like(lanes))
        groups.append(jnp.sum(picked, axis=0, keepdims=True))
    return jnp.concatenate(groups, axis=1)


def kernel(n_mon, n_sub, chunk, df_hbm, mask_hbm, base_hbm, row_hbm, pair_hbm, count_hbm, out_v,
           own_df, rest_df, far_df, mask_v, far_mask, base_v, row_v, pair_v, count_s,
           base_wide, product, mask_sum, flow_own, flow_got, cross_own, cross_got,
           load_sem, part_send, part_recv, flow_send, flow_recv, cross_send, cross_recv):
    rows_dev, width = df_hbm.shape
    half = rows_dev // n_sub
    blocks = half // BLOCK
    capacity = pair_hbm.shape[1]
    chunks = capacity // chunk
    n = n_mon * n_sub
    mon = lax.axis_index("mon")
    sub = lax.axis_index("sub")
    me = mon * n_sub + sub
    other = 1 - sub

    def peer(step):
        flat = lax.rem(me + step, n)
        return {"mon": flat // n_sub, "sub": lax.rem(flat, n_sub)}

    barrier = pltpu.get_barrier_semaphore()

    def greet(step, carry):
        pl.semaphore_signal(barrier, inc=1, device_id=peer(step), device_id_type=MESH)
        return carry

    lax.fori_loop(1, n, greet, 0)

    loads = [
        pltpu.make_async_copy(pair_hbm, pair_v, load_sem.at[0]),
        pltpu.make_async_copy(row_hbm, row_v, load_sem.at[1]),
        pltpu.make_async_copy(df_hbm.at[pl.ds(sub * half, half)], own_df, load_sem.at[2]),
        pltpu.make_async_copy(base_hbm.at[pl.ds(sub * blocks, blocks)], base_v, load_sem.at[3]),
        pltpu.make_async_copy(df_hbm.at[pl.ds(other * half, half)], rest_df.at[pl.ds(0, half)], load_sem.at[4]),
        pltpu.make_async_copy(mask_hbm, mask_v, load_sem.at[5]),
        pltpu.make_async_copy(count_hbm, count_s, load_sem.at[6]),
    ]
    for load in loads:
        load.start()
    loads[0].wait()
    loads[1].wait()
    loads[3].wait()
    table = row_v[...]
    base = base_v[...]
    first, second = pair_v[0:1, :], pair_v[1:2, :]
    first_row, second_row = lookup(table, first), lookup(table, second)
    row_start = mon * rows_dev
    flow_start = row_start + sub * half
    flow_own[0:1, :] = lookup(base, first_row - flow_start)
    flow_own[1:2, :] = lookup(base, second_row - flow_start)
    for b in range(blocks):
        base_wide[b * BLOCK:(b + 1) * BLOCK, :] = jnp.broadcast_to(base[b:b + 1, :], (BLOCK, BLOCK)).T

    pl.semaphore_wait(barrier, n - 1)
    partner = {"sub": other}
    part_copies = [
        pltpu.make_async_remote_copy(
            df_hbm.at[pl.ds(other * half, half)], far_df.at[pl.ds(0, half)],
            part_send.at[0], part_recv.at[0], device_id=partner, device_id_type=MESH),
        pltpu.make_async_remote_copy(
            mask_hbm.at[pl.ds(other * blocks, blocks)], far_mask,
            part_send.at[1], part_recv.at[1], device_id=partner, device_id_type=MESH),
    ]
    for copy in part_copies:
        copy.start()

    def send_flow(step, carry):
        pltpu.make_async_remote_copy(
            flow_own, flow_got.at[step - 1], flow_send, flow_recv,
            device_id=peer(step), device_id_type=MESH).start()
        return carry

    lax.fori_loop(1, n, send_flow, 0)

    def send_cross(c):
        def body(step, carry):
            pltpu.make_async_remote_copy(
                cross_own.at[c], cross_got.at[c, step - 1], cross_send.at[c], cross_recv.at[c],
                device_id=peer(step), device_id_type=MESH).start()
            return carry

        lax.fori_loop(1, n, body, 0)

    def both(left, right, c):
        span = slice(c * chunk, (c + 1) * chunk)
        return jnp.concatenate([left[:, span], right[:, span]], axis=1)

    def one_hot(columns, start):
        level = lax.broadcasted_iota(I32, (width, columns.shape[1]), 0) + start
        return jnp.where(level == columns, F32(1), F32(0)).astype(BF16)

    loads[5].wait()
    rest_df[half:, :] = mask_v[...].astype(F32).astype(BF16)
    loads[2].wait()
    loads[4].wait()
    level = lax.broadcasted_iota(I32, (half, 2 * chunk), 0)
    level16 = lax.broadcasted_iota(I32, (n_sub * blocks, 2 * chunk), 0)
    for c in range(chunks):
        columns = both(first, second, c)
        wanted = both(second_row, first_row, c) - row_start
        hot = one_hot(columns, sub * width)
        near = jnp.dot(own_df[...], hot, preferred_element_type=F32)
        product[c] = near.astype(BF16)
        found = jnp.sum(jnp.where(level == wanted - sub * half, near, F32(0)), axis=0, keepdims=True)
        rest = jnp.dot(rest_df[...], hot, preferred_element_type=F32)
        found = found + jnp.sum(
            jnp.where(level == wanted - other * half, rest[:half], F32(0)), axis=0, keepdims=True)
        kept = rest[half:]
        keep = jnp.sum(jnp.where(level16 == (wanted >> 7), kept, F32(0)), axis=0, keepdims=True)
        mask_sum[c] = jnp.where(sub == 0, kept[:blocks], kept[blocks:])
        found = found * keep
        cross_own[c, 0:1, :] = found[:, chunk:]
        cross_own[c, 1:2, :] = found[:, :chunk]
        send_cross(c)

    for copy in part_copies:
        copy.wait_recv()
    far_df[half:half + blocks, :] = far_mask[...].astype(F32).astype(BF16)
    for c in range(chunks):
        hot = one_hot(both(first, second, c), other * width)
        far = jnp.dot(far_df[...], hot, preferred_element_type=F32)
        product[c] = (product[c].astype(F32) + far[:half]).astype(BF16)
        mask_sum[c] = mask_sum[c] + far[half:half + blocks]

    pltpu.make_async_copy(flow_got, flow_got, flow_recv).wait()
    loads[6].wait()
    flow = flow_own[...] + jnp.sum(flow_got[...], axis=0)
    live = (lax.broadcasted_iota(I32, (1, capacity), 1) < count_s[0]).astype(F32)
    for c in range(chunks):
        span = slice(c * chunk, (c + 1) * chunk)
        pltpu.make_async_copy(cross_got.at[c], cross_got.at[c], cross_recv.at[c]).wait()
        cross = cross_own[c] + jnp.sum(cross_got[c], axis=0)
        cross_first, cross_second = cross[0:1], cross[1:2]
        flow_first, flow_second = flow[0:1, span], flow[1:2, span]
        determinant = 1.0 - cross_first * cross_second
        shift_first = (flow_first + cross_first * flow_second) / determinant
        shift_second = (flow_second + cross_second * flow_first) / determinant
        alive = live[:, span]
        shift_first = shift_first.astype(BF16).astype(F32) * alive
        shift_second = shift_second.astype(BF16).astype(F32) * alive
        keep = mask_sum[c]
        for b in range(blocks):
            rows = slice(b * BLOCK, (b + 1) * BLOCK)
            flows = jnp.concatenate([base_wide[rows, :]] * (chunk // BLOCK), axis=1)
            e1 = shift_first * keep[b:b + 1, :chunk]
            e2 = shift_second * keep[b:b + 1, chunk:]
            value = flows * alive + product[c, rows, :chunk].astype(F32) * e1
            value = value + product[c, rows, chunk:].astype(F32) * e2
            out_v[rows, span] = value.astype(BF16)

    for copy in part_copies:
        copy.wait_send()
    pltpu.make_async_copy(flow_got, flow_got, flow_send).wait()
    for c in range(chunks):
        pltpu.make_async_copy(cross_got.at[c], cross_got.at[c], cross_send.at[c]).wait()


def on_device(n_mon, n_sub, dfactors, block_mask, base_flow, branch_row, pair_slots, pair_counts):
    rows_dev, width = dfactors.shape
    half = rows_dev // n_sub
    blocks = half // BLOCK
    capacity = pair_slots.shape[0]
    chunk = 256 if capacity % 256 == 0 else BLOCK
    chunks = capacity // chunk
    n = n_mon * n_sub
    any_spec = pl.BlockSpec(memory_space=pltpu.HBM)
    dma = pltpu.SemaphoreType.DMA
    made = pl.pallas_call(
        functools.partial(kernel, n_mon, n_sub, chunk),
        out_shape=pltpu.VMEM((half, capacity), BF16),
        in_specs=[any_spec] * 6,
        out_specs=pl.BlockSpec(memory_space=pltpu.VMEM),
        scratch_shapes=[
            pltpu.VMEM((half, width), BF16),
            pltpu.VMEM((half + n_sub * blocks, width), BF16),
            pltpu.VMEM((half + n_sub * blocks, width), BF16),
            pltpu.VMEM((n_sub * blocks, width), I32),
            pltpu.VMEM((blocks, width), I32),
            pltpu.VMEM((blocks, BLOCK), F32),
            pltpu.VMEM((branch_row.shape[0] // BLOCK, BLOCK), I32),
            pltpu.VMEM((2, capacity), I32),
            pltpu.SMEM((1,), I32),
            pltpu.VMEM((half, BLOCK), F32),
            pltpu.VMEM((chunks, half, 2 * chunk), BF16),
            pltpu.VMEM((chunks, blocks, 2 * chunk), F32),
            pltpu.VMEM((2, capacity), F32),
            pltpu.VMEM((n - 1, 2, capacity), F32),
            pltpu.VMEM((chunks, 2, chunk), F32),
            pltpu.VMEM((chunks, n - 1, 2, chunk), F32),
            dma((7,)), dma((2,)), dma((2,)), dma, dma, dma((chunks,)), dma((chunks,)),
        ],
        compiler_params=pltpu.CompilerParams(
            collective_id=0, has_side_effects=True, vmem_limit_bytes=60 * 1024 * 1024),
    )(dfactors, block_mask, base_flow.reshape(-1, BLOCK), branch_row.reshape(-1, BLOCK),
      pair_slots.T, pair_counts)
    return made


def solution(mesh):
    return jax.shard_map(
        functools.partial(on_device, mesh.shape["mon"], mesh.shape["sub"]),
        mesh=mesh,
        in_specs=(
            P("mon", "sub"),
            P("mon", "sub"),
            P("mon"),
            P(),
            P(("grp", "pair"), None),
            P(("grp", "pair")),
        ),
        out_specs=P(("mon", "sub"), ("grp", "pair")),
        check_vma=False,
    )
```

```python
import functools

import jax
import jax.numpy as jnp
from jax import lax
from jax.experimental import pallas as pl
from jax.experimental.pallas import tpu as pltpu
from jax.sharding import PartitionSpec as P

BLOCK = 128
MESH = pl.DeviceIdType.MESH
F32 = jnp.float32
BF16 = jnp.bfloat16
I32 = jnp.int32


def lookup(table, index):
    groups = []
    height = table.shape[0]
    for start in range(0, index.shape[1], 128):
        wide = jnp.broadcast_to(index[:, start:start + 128], (height, 128))
        lanes = jnp.take_along_axis(table, wide & 127, axis=1)
        level = lax.broadcasted_iota(I32, (height, 128), 0)
        picked = jnp.where(level == (wide >> 7), lanes, jnp.zeros_like(lanes))
        groups.append(jnp.sum(picked, axis=0, keepdims=True))
    return jnp.concatenate(groups, axis=1)


def flows_of(b, base_wide, product, effect, alive):
    rows = slice(b * BLOCK, (b + 1) * BLOCK)
    chunk = product.shape[1] // 2
    flows = jnp.concatenate([base_wide[rows, :]] * (chunk // BLOCK), axis=1)
    value = flows * alive + product[rows, :chunk].astype(F32) * effect[b:b + 1, :chunk]
    value = value + product[rows, chunk:].astype(F32) * effect[b:b + 1, chunk:]
    return value.astype(BF16)


def last_kernel(pieces, ready, product, effect, base_wide, alive, out_hbm, last, sems):
    chunks, half, pair_width = product.shape
    chunk = pair_width // 2
    split = (chunks - 1) * chunk
    rows = half // pieces
    copies = []
    if chunks > 1:
        for piece in range(2):
            span = pl.ds(piece * (half // 2), half // 2)
            columns = pl.ds(0, split)
            copies.append(pltpu.make_async_copy(
                ready.at[span, columns], out_hbm.at[span, columns], sems.at[pieces + piece]))
            copies[-1].start()
    for piece in range(pieces):
        for b in range(piece * rows // BLOCK, (piece + 1) * rows // BLOCK):
            last[b * BLOCK:(b + 1) * BLOCK, :] = flows_of(
                b, base_wide, product.at[chunks - 1], effect, alive[...])
        span = pl.ds(piece * rows, rows)
        copies.append(pltpu.make_async_copy(
            last.at[span], out_hbm.at[span, pl.ds(split, chunk)], sems.at[piece]))
        copies[-1].start()
    for copy in copies:
        copy.wait()


def kernel(n_mon, n_sub, chunk, df_hbm, mask_hbm, base_hbm, row_hbm, pair_hbm, count_hbm, out_v, product, effect, base_wide, alive_v,
           own_df, rest_df, far_df, mask_v, far_mask, base_v, row_v, pair_v, count_s,
           mask_sum, flow_own, flow_got, cross_own, cross_got,
           load_sem, part_send, part_recv, flow_send, flow_recv, cross_send, cross_recv):
    rows_dev, width = df_hbm.shape
    half = rows_dev // n_sub
    blocks = half // BLOCK
    capacity = pair_hbm.shape[1]
    chunks = capacity // chunk
    n = n_mon * n_sub
    mon = lax.axis_index("mon")
    sub = lax.axis_index("sub")
    me = mon * n_sub + sub
    other = 1 - sub

    def peer(step):
        flat = lax.rem(me + step, n)
        return {"mon": flat // n_sub, "sub": lax.rem(flat, n_sub)}

    barrier = pltpu.get_barrier_semaphore()

    def greet(step, carry):
        pl.semaphore_signal(barrier, inc=1, device_id=peer(step), device_id_type=MESH)
        return carry

    lax.fori_loop(1, n, greet, 0)

    loads = [
        pltpu.make_async_copy(pair_hbm, pair_v, load_sem.at[0]),
        pltpu.make_async_copy(row_hbm, row_v, load_sem.at[1]),
        pltpu.make_async_copy(df_hbm.at[pl.ds(sub * half, half)], own_df, load_sem.at[2]),
        pltpu.make_async_copy(base_hbm.at[pl.ds(sub * blocks, blocks)], base_v, load_sem.at[3]),
        pltpu.make_async_copy(df_hbm.at[pl.ds(other * half, half)], rest_df.at[pl.ds(0, half)], load_sem.at[4]),
        pltpu.make_async_copy(mask_hbm, mask_v, load_sem.at[5]),
        pltpu.make_async_copy(count_hbm, count_s, load_sem.at[6]),
    ]
    for load in loads:
        load.start()
    loads[0].wait()
    loads[1].wait()
    loads[3].wait()
    table = row_v[...]
    base = base_v[...]
    first, second = pair_v[0:1, :], pair_v[1:2, :]
    first_row, second_row = lookup(table, first), lookup(table, second)
    row_start = mon * rows_dev
    flow_start = row_start + sub * half
    flow_own[0:1, :] = lookup(base, first_row - flow_start)
    flow_own[1:2, :] = lookup(base, second_row - flow_start)

    partner = {"sub": other}
    part_copies = [
        pltpu.make_async_remote_copy(
            df_hbm.at[pl.ds(other * half, half)], far_df.at[pl.ds(0, half)],
            part_send.at[0], part_recv.at[0], device_id=partner, device_id_type=MESH),
        pltpu.make_async_remote_copy(
            mask_hbm.at[pl.ds(other * blocks, blocks)], far_mask,
            part_send.at[1], part_recv.at[1], device_id=partner, device_id_type=MESH),
    ]
    def send_flow(step, carry):
        pltpu.make_async_remote_copy(
            flow_own, flow_got.at[step - 1], flow_send, flow_recv,
            device_id=peer(step), device_id_type=MESH).start()
        return carry

    pl.semaphore_wait(barrier, n - 1)
    for copy in part_copies:
        copy.start()
    lax.fori_loop(1, n, send_flow, 0)

    def send_cross(c):
        def body(step, carry):
            pltpu.make_async_remote_copy(
                cross_own.at[c], cross_got.at[c, step - 1], cross_send.at[c], cross_recv.at[c],
                device_id=peer(step), device_id_type=MESH).start()
            return carry

        lax.fori_loop(1, n, body, 0)

    def both(left, right, c):
        span = slice(c * chunk, (c + 1) * chunk)
        return jnp.concatenate([left[:, span], right[:, span]], axis=1)

    def one_hot(columns, start):
        level = lax.broadcasted_iota(I32, (width, columns.shape[1]), 0) + start
        return jnp.where(level == columns, F32(1), F32(0)).astype(BF16)

    loads[5].wait()
    rest_df[half:, :] = mask_v[...].astype(F32).astype(BF16)
    loads[2].wait()
    level = lax.broadcasted_iota(I32, (half, 2 * chunk), 0)
    level16 = lax.broadcasted_iota(I32, (n_sub * blocks, 2 * chunk), 0)
    for c in range(chunks):
        columns = both(first, second, c)
        wanted = both(second_row, first_row, c) - row_start
        hot = one_hot(columns, sub * width)
        near = jnp.dot(own_df[...], hot, preferred_element_type=F32)
        product[c] = near.astype(BF16)
        found = jnp.sum(jnp.where(level == wanted - sub * half, near, F32(0)), axis=0, keepdims=True)
        if c == 0:
            loads[4].wait()
        rest = jnp.dot(rest_df[...], hot, preferred_element_type=F32)
        found = found + jnp.sum(
            jnp.where(level == wanted - other * half, rest[:half], F32(0)), axis=0, keepdims=True)
        kept = rest[half:]
        keep = jnp.sum(jnp.where(level16 == (wanted >> 7), kept, F32(0)), axis=0, keepdims=True)
        mask_sum[c] = jnp.where(sub == 0, kept[:blocks], kept[blocks:])
        found = found * keep
        cross_own[c, 0:1, :] = found[:, chunk:]
        cross_own[c, 1:2, :] = found[:, :chunk]
        send_cross(c)
    for b in range(blocks):
        base_wide[b * BLOCK:(b + 1) * BLOCK, :] = jnp.broadcast_to(base[b:b + 1, :], (BLOCK, BLOCK)).T

    for copy in part_copies:
        copy.wait_recv()
    far_df[half:half + blocks, :] = far_mask[...].astype(F32).astype(BF16)
    for c in range(chunks):
        hot = one_hot(both(first, second, c), other * width)
        far = jnp.dot(far_df[...], hot, preferred_element_type=F32)
        product[c] = (product[c].astype(F32) + far[:half]).astype(BF16)
        mask_sum[c] = mask_sum[c] + far[half:half + blocks]

    pltpu.make_async_copy(flow_got, flow_got, flow_recv).wait()
    loads[6].wait()
    flow = flow_own[...] + jnp.sum(flow_got[...], axis=0)
    live = (lax.broadcasted_iota(I32, (1, capacity), 1) < count_s[0]).astype(F32)
    for c in range(chunks):
        span = slice(c * chunk, (c + 1) * chunk)
        pltpu.make_async_copy(cross_got.at[c], cross_got.at[c], cross_recv.at[c]).wait()
        cross = cross_own[c] + jnp.sum(cross_got[c], axis=0)
        cross_first, cross_second = cross[0:1], cross[1:2]
        flow_first, flow_second = flow[0:1, span], flow[1:2, span]
        determinant = 1.0 - cross_first * cross_second
        shift_first = (flow_first + cross_first * flow_second) / determinant
        shift_second = (flow_second + cross_second * flow_first) / determinant
        alive = live[:, span]
        shift_first = shift_first.astype(BF16).astype(F32) * alive
        shift_second = shift_second.astype(BF16).astype(F32) * alive
        keep = mask_sum[c]
        effect[:, :chunk] = shift_first * keep[:, :chunk]
        effect[:, chunk:] = shift_second * keep[:, chunk:]
        if c == chunks - 1:
            alive_v[...] = alive
        else:
            for b in range(blocks):
                rows = slice(b * BLOCK, (b + 1) * BLOCK)
                out_v[rows, span] = flows_of(b, base_wide, product.at[c], effect, alive)

    for copy in part_copies:
        copy.wait_send()
    pltpu.make_async_copy(flow_got, flow_got, flow_send).wait()
    for c in range(chunks):
        pltpu.make_async_copy(cross_got.at[c], cross_got.at[c], cross_send.at[c]).wait()


def on_device(n_mon, n_sub, dfactors, block_mask, base_flow, branch_row, pair_slots, pair_counts):
    rows_dev, width = dfactors.shape
    half = rows_dev // n_sub
    blocks = half // BLOCK
    capacity = pair_slots.shape[0]
    chunk = 256 if capacity % 256 == 0 else BLOCK
    chunks = capacity // chunk
    n = n_mon * n_sub
    any_spec = pl.BlockSpec(memory_space=pltpu.HBM)
    vmem_spec = pl.BlockSpec(memory_space=pltpu.VMEM)
    dma = pltpu.SemaphoreType.DMA
    made = pl.pallas_call(
        functools.partial(kernel, n_mon, n_sub, chunk),
        out_shape=[
            pltpu.VMEM((half, capacity), BF16),
            pltpu.VMEM((chunks, half, 2 * chunk), BF16),
            pltpu.VMEM((blocks, 2 * chunk), F32),
            pltpu.VMEM((half, BLOCK), F32),
            pltpu.VMEM((1, chunk), F32),
        ],
        in_specs=[any_spec] * 6,
        out_specs=[vmem_spec] * 5,
        scratch_shapes=[
            pltpu.VMEM((half, width), BF16),
            pltpu.VMEM((half + n_sub * blocks, width), BF16),
            pltpu.VMEM((half + n_sub * blocks, width), BF16),
            pltpu.VMEM((n_sub * blocks, width), I32),
            pltpu.VMEM((blocks, width), I32),
            pltpu.VMEM((blocks, BLOCK), F32),
            pltpu.VMEM((branch_row.shape[0] // BLOCK, BLOCK), I32),
            pltpu.VMEM((2, capacity), I32),
            pltpu.SMEM((1,), I32),
            pltpu.VMEM((chunks, blocks, 2 * chunk), F32),
            pltpu.VMEM((2, capacity), F32),
            pltpu.VMEM((n - 1, 2, capacity), F32),
            pltpu.VMEM((chunks, 2, chunk), F32),
            pltpu.VMEM((chunks, n - 1, 2, chunk), F32),
            dma((7,)), dma((2,)), dma((2,)), dma, dma, dma((chunks,)), dma((chunks,)),
        ],
        compiler_params=pltpu.CompilerParams(
            collective_id=0, has_side_effects=True, vmem_limit_bytes=int(58.8 * 1024 * 1024)),
    )(dfactors, block_mask, base_flow.reshape(-1, BLOCK), branch_row.reshape(-1, BLOCK),
      pair_slots.T, pair_counts)
    pieces = 2
    return pl.pallas_call(
        functools.partial(last_kernel, pieces),
        out_shape=jax.ShapeDtypeStruct((half, capacity), BF16),
        in_specs=[vmem_spec] * 5,
        out_specs=any_spec,
        scratch_shapes=[pltpu.VMEM((half, chunk), BF16), dma((pieces + 2,))],
        compiler_params=pltpu.CompilerParams(vmem_limit_bytes=8 * 1024 * 1024),
    )(*[pltpu.with_memory_space_constraint(array, pltpu.VMEM) for array in made])


def solution(mesh):
    return jax.shard_map(
        functools.partial(on_device, mesh.shape["mon"], mesh.shape["sub"]),
        mesh=mesh,
        in_specs=(
            P("mon", "sub"),
            P("mon", "sub"),
            P("mon"),
            P(),
            P(("grp", "pair"), None),
            P(("grp", "pair")),
        ),
        out_specs=P(("mon", "sub"), ("grp", "pair")),
        check_vma=False,
    )
```
